32 devices in a mesh: mem: 4 (over z), slab: 8 (over y, x, core).
Axes of the slice: x: 2, y: 2, z: 4, core: 2. Of those that a mesh axis runs over, the one named last changes fastest.
Arguments:
- ensemble: float32 [256, 256, 128], P('mem', 'slab'), may hold values from -6 to 6
- diffusivity: float32 [256, 128], P('slab'), may hold values from 0.15 to 0.25
- velocity: float32 [2, 256, 128], P(None, 'slab'), may hold values from -0.5 to 0.5
- obs_value: float32 [40960], P(('mem', 'slab')), may hold values from -6 to 6
- obs_weight: float32 [40960], P(('mem', 'slab')), may hold values from 0.3 to 12
- obs_slab: int32 [40960, 1], P(('mem', 'slab')), may hold values from 0 to 7; in each aligned block of 1280 rows (0 to 1279, 1280 to 2559, ...) at most 320 rows name the same one
- obs_cell: int32 [40960], P(('mem', 'slab')), may hold values from 0 to 1023
Outputs:
- analysis: float32 [256, 256, 128], P('mem', 'slab')
The draws below stay inside these ranges and needn't reach their ends.
Inputs may be any that keep to these rules, and one draw needn't show every extreme that they name: `obs_slab`: among the 1280 observations stored on one device, no slab is named more than 320 times; on some device one slab is named exactly 320 times.
All inputs are finite; a program needn't handle non-finite values.
Results may differ from the reference program's by a relative error of at most 0.0085.
Values sent between devices are 32-bit elements; how exact they have to be, the bound alone decides.
No kernel may reach another device: no remote copies, remote signals or barrier semaphores. Data moves between devices by JAX's collectives and lax.ppermute only.
A program may use at most 128 MiB of HBM per device.

```python
import math
import jax
import jax.numpy as jnp
import numpy as np
from jax import lax

M = 256
GX = 128
PATCH_DEV = 8
STEPS = 4
NS_STEPS = 5
OBS_DEV = 1280
CAP = 320
ROWS_DEV = 32
GY = 256
NOBS = 40960
N_MEM = 4
N_SLAB = 8


def with_ends(array, own_key, smallest, largest):
    index_at = [jax.random.randint(jax.random.fold_in(own_key, axis), (), 0, length) for axis, length in enumerate(array.shape)]
    longest = array.shape.index(max(array.shape))
    neighbour = index_at[:longest] + [(index_at[longest] + 1) % array.shape[longest]] + index_at[longest + 1:]
    return array.at[tuple(index_at)].set(smallest).at[tuple(neighbour)].set(largest)


def levels(stream_key, shape, split, smallest, high):
    gain = 1.0
    for axis_at, parts in split:
        steps = jax.random.uniform(jax.random.fold_in(jax.random.fold_in(stream_key, 6), axis_at), (parts,), jnp.float32, smallest / len(split), high / len(split))
        gain = gain * jnp.repeat(jnp.exp(steps), shape[axis_at] // parts).reshape((-1,) + (1,) * (len(shape) - 1 - axis_at))
    return gain


def routed_block(own_key, own, number, rows, count, top, bound, lean):
    sequence = jax.random.permutation(own_key, count)
    packed, ordinary = portions_of(count, rows * top, bound, lean, True), portions_of(count, rows * top, bound, lean, False)
    places = jnp.arange(count)

    def named(tallies, turn):
        used = int((tallies > 0).sum())
        fixed = max(1, used // 4)
        passed = fixed + (places - fixed + turn * (used - fixed)) % max(1, count - fixed)
        return jnp.zeros((count,), jnp.int32).at[sequence[jnp.where(places < fixed, places, passed)]].set(jnp.asarray(tallies, jnp.int32))

    tallies = jnp.where(number % 4 == 0, named(packed, number // 4), named(ordinary, number - number // 4 - 1))
    mixed = jax.random.permutation(jax.random.fold_in(own, 3), count)
    donor, taker = mixed[0:count // 2 * 2:2], mixed[1:count // 2 * 2:2]
    slack = jnp.minimum(tallies[donor] - 1, bound - tallies[taker]) // 2
    slack = jnp.where((donor == sequence[0]) | (taker == sequence[0]) | (tallies[taker] == 0), 0, jnp.maximum(slack, 0))
    passed = jax.random.randint(jax.random.fold_in(own, 4), (count // 2,), 0, 1 << 20) % (slack + 1)
    tallies = tallies.at[donor].add(-passed).at[taker].add(passed)
    labels = jnp.searchsorted(jnp.cumsum(tallies), jnp.arange(rows * top), side="right").astype(jnp.int32)
    table = labels.reshape(top, rows).T
    table = table[jax.random.permutation(jax.random.fold_in(own, 1), rows)]
    turn = jax.random.randint(jax.random.fold_in(own, 2), (rows, 1), 0, top)
    return jnp.take_along_axis(table, (jnp.arange(top)[None, :] + turn) % top, axis=1)


def portions_of(count, total, reach, lean, full):
    weights = [(1 << 20) // math.isqrt(standing ** lean) + 1 for standing in range(1, count + 1)]
    largest = reach if full else min(reach, max(-(-total // count), total * weights[0] // sum(weights)))
    least = 1 if total - largest >= count - 1 else 0
    given, spare = [largest] + [least] * (count - 1), total - largest - least * (count - 1)
    while spare > 0:
        free = [i for i in range(1, count) if given[i] < largest] or [i for i in range(1, count) if given[i] < reach]
        pool, budget = sum([weights[i] for i in free]), spare
        for i in free:
            extra = min(reach - given[i], max(1, budget * weights[i] // pool), spare)
            given[i] = given[i] + extra
            spare = spare - extra
    return np.array(given)


def gaussian(key, extent, deviation, limit, split=(), held_as=jnp.bfloat16):
    array = deviation * jax.random.normal(key, extent, jnp.float32)
    if split:
        array = array * levels(key, extent, split, -0.22, 0.18)
    return jnp.clip(array, -limit, limit).astype(held_as)


def setup_inputs(seed: int = 0) -> dict:
    splits = jax.random.split(jax.random.key(seed), 8)
    ensemble = gaussian(splits[0], (M, GY, GX), 1.0, 6.0, ((0, 4), (1, 8)), jnp.float32)
    diffusivity = jnp.clip(0.15 + 0.099999994 * jax.random.uniform(splits[1], (GY, GX), jnp.float32) ** levels(splits[1], (GY, GX), ((0, 8),), -0.2, 0.2), 0.15, 0.25)
    velocity = jnp.clip(jax.random.uniform(splits[2], (2, GY, GX), jnp.float32, -0.5, 0.5) * levels(splits[2], (2, GY, GX), ((1, 8),), -0.4, 0.0), -0.5, 0.5)
    obs_value = gaussian(splits[3], (NOBS,), 1.0, 6.0, ((0, 32),), jnp.float32)
    obs_weight = jnp.clip(jnp.exp(math.log(12.0) - 3.6888794 * jax.random.uniform(splits[4], (NOBS,), jnp.float32) ** levels(splits[4], (NOBS,), ((0, 32),), -0.2, 0.2)), 0.3, 12.0)
    obs_slab_keys = jax.random.split(jax.random.fold_in(splits[5], 1), NOBS // OBS_DEV)
    obs_slab_turns = jax.random.permutation(jax.random.fold_in(splits[5], 3), NOBS // OBS_DEV)
    obs_slab = jax.vmap(lambda own, number: routed_block(jax.random.fold_in(splits[5], 2), own, number, OBS_DEV, N_SLAB, 1, CAP, 2))(obs_slab_keys, obs_slab_turns).reshape((NOBS, 1))
    obs_cell = with_ends(jax.random.randint(splits[6], (NOBS,), 0, PATCH_DEV * GX), jax.random.fold_in(splits[6], 1), 0, (PATCH_DEV * GX) - 1).astype(jnp.int32)
    return dict(ensemble=ensemble, diffusivity=diffusivity, velocity=velocity, obs_value=obs_value, obs_weight=obs_weight, obs_slab=obs_slab, obs_cell=obs_cell)


def stencil(center, upper_row, lower_row, diffuse, drift_x, drift_y):
    east_side = jnp.roll(center, -1, axis=-1)
    west_side = jnp.roll(center, 1, axis=-1)
    laplace = east_side + west_side + upper_row + lower_row - 4.0 * center
    return center + diffuse * laplace - 0.5 * drift_x * (east_side - west_side) - 0.5 * drift_y * (lower_row - upper_row)

def analyse(fields, obs_vals, obs_wts, obs_cells):
    members, patches, width = fields.shape
    center_mean = lax.optimization_barrier(jnp.mean(fields, axis=0))
    spread = (fields - center_mean[None]).astype(jnp.bfloat16)
    flat_mean = center_mean.reshape(-1)
    at_obs = jnp.take(spread.reshape(members, -1), obs_cells, axis=1)
    misfit = obs_vals - jnp.take(flat_mean, obs_cells)
    patch_of = obs_cells // width
    weights = obs_wts[None, :] * (patch_of[None, :] == jnp.arange(patches, dtype=jnp.int32)[:, None]).astype(jnp.float32)
    weighted = (at_obs[None].astype(jnp.float32) * weights[:, None, :]).astype(jnp.bfloat16)
    gram = jnp.einsum('pmo,no->pmn', weighted.astype(jnp.float32), at_obs.astype(jnp.float32), precision=lax.Precision.HIGHEST)
    eye_f = jnp.eye(members, dtype=jnp.float32)
    system = (members - 1) * eye_f[None] + gram
    scale = 8.0 * jnp.sqrt(lax.optimization_barrier(jnp.sum(system * system, axis=(1, 2))) / members)
    iterate = (system / scale[:, None, None]).astype(jnp.bfloat16)
    inverse_root = jnp.broadcast_to(eye_f.astype(jnp.bfloat16), iterate.shape)
    for sweep in range(NS_STEPS):
        product = jnp.einsum('pij,pjk->pik', inverse_root.astype(jnp.float32), iterate.astype(jnp.float32), precision=lax.Precision.HIGHEST)
        factor = (1.5 * eye_f[None] - 0.5 * product).astype(jnp.bfloat16)
        iterate = jnp.einsum('pij,pjk->pik', iterate.astype(jnp.float32), factor.astype(jnp.float32), precision=lax.Precision.HIGHEST).astype(jnp.bfloat16)
        inverse_root = jnp.einsum('pij,pjk->pik', factor.astype(jnp.float32), inverse_root.astype(jnp.float32), precision=lax.Precision.HIGHEST).astype(jnp.bfloat16)
    root_f = inverse_root.astype(jnp.float32)
    pull = jnp.dot(at_obs.astype(jnp.float32), (weights * misfit[None, :]).T, precision=lax.Precision.HIGHEST)
    first = jnp.einsum('pij,jp->pi', root_f, pull, precision=lax.Precision.HIGHEST)
    mean_gain = jnp.einsum('pij,pj->pi', root_f, first, precision=lax.Precision.HIGHEST) / scale[:, None]
    transform = (jnp.sqrt((members - 1) / scale)[:, None, None] * root_f + mean_gain[:, None, :]).astype(jnp.bfloat16)
    update = jnp.einsum('pik,kpx->ipx', transform.astype(jnp.float32), spread.astype(jnp.float32), precision=lax.Precision.HIGHEST)
    return center_mean[None] + update

def reference(ensemble, diffusivity, velocity, obs_value, obs_weight, obs_slab, obs_cell):
    fields = ensemble
    for step in range(STEPS):
        fields = stencil(fields, jnp.roll(fields, 1, axis=1), jnp.roll(fields, -1, axis=1), diffusivity, velocity[0], velocity[1])
    row_vals = obs_value.reshape(N_MEM, N_SLAB * OBS_DEV)
    row_wts = obs_weight.reshape(N_MEM, N_SLAB * OBS_DEV)
    row_slab = obs_slab[:, 0].reshape(N_MEM, N_SLAB * OBS_DEV)
    row_cell = obs_cell.reshape(N_MEM, N_SLAB * OBS_DEV)

    def one_device(index):
        mem_id = index // N_SLAB
        slab_id = index % N_SLAB
        start = (slab_id * ROWS_DEV + mem_id * PATCH_DEV).astype(jnp.int32)
        block = lax.dynamic_slice_in_dim(fields, start, PATCH_DEV, 1)
        wanted = row_slab[mem_id] == slab_id
        ranking = jnp.argsort(1 - wanted.astype(jnp.int32), stable=True)[:N_SLAB * CAP]
        keep = wanted[ranking]
        obs_vals = jnp.where(keep, row_vals[mem_id][ranking], 0.0)
        obs_wts = jnp.where(keep, row_wts[mem_id][ranking], 0.0)
        obs_cells = jnp.where(keep, row_cell[mem_id][ranking], 0).astype(jnp.int32)
        return analyse(block, obs_vals, obs_wts, obs_cells)
    stacked = lax.map(one_device, jnp.arange(N_MEM * N_SLAB, dtype=jnp.int32))
    return stacked.reshape(N_MEM, N_SLAB, M, PATCH_DEV, GX).transpose(2, 1, 0, 3, 4).reshape(M, GY, GX)
```

```python
import functools

import jax
import jax.numpy as jnp
from jax import lax
from jax.experimental import pallas as pl
from jax.experimental.pallas import tpu as pltpu
from jax.sharding import PartitionSpec as P

STEPS = 4
NS_STEPS = 5
HALF = 4
SUB = 8
F32 = jnp.float32
BF16 = jnp.bfloat16

VMEM = pl.BlockSpec(memory_space=pltpu.VMEM)
SMEM = pl.BlockSpec(memory_space=pltpu.SMEM)


def edge_kernel(top_ref, bottom_ref, coef_ref, head_ref, tail_ref):
    members = top_ref.shape[0]
    rows = coef_ref.shape[1]
    for r in range(STEPS):
        head_ref[r, :members, :] = top_ref[:, 0, r, :]
        tail_ref[r, :members, :] = bottom_ref[:, 0, SUB - STEPS + r, :]
        for k in range(3):
            head_ref[r, members + k : members + k + 1, :] = coef_ref[k, r : r + 1, :]
            tail_ref[r, members + k : members + k + 1, :] = coef_ref[
                k, rows - STEPS + r : rows - STEPS + r + 1, :
            ]


def edges(ens, coefs):
    members, groups = ens.shape[:2]
    width = ens.shape[-1]
    shape = jax.ShapeDtypeStruct((STEPS, members + SUB, width), F32)
    block = (members, 1, SUB, width)
    return pl.pallas_call(
        edge_kernel,
        grid=(1,),
        in_specs=[
            pl.BlockSpec(block, lambda i: (0, 0, 0, 0)),
            pl.BlockSpec(block, lambda i: (0, groups - 1, 0, 0)),
            pl.BlockSpec(coefs.shape, lambda i: (0, 0, 0)),
        ],
        out_specs=[pl.BlockSpec(shape.shape, lambda i: (0, 0, 0))] * 2,
        out_shape=[shape] * 2,
        name="edges",
    )(ens, ens, coefs)


def forecast_kernel(chunk, n_mem, *refs):
    if chunk:
        place, ens_ref, coef_ref, above_ref, below_ref = refs[:5]
        refs = refs[5:]
    else:
        place, ens_ref, coef_ref = refs[:3]
        refs = refs[3:]
    outs, field, table = refs[:n_mem], refs[n_mem], refs[n_mem + 1]
    members, groups, _, width = ens_ref.shape
    rows = groups * SUB

    for g in range(groups):
        for r in range(SUB):
            field[STEPS + g * SUB + r] = ens_ref[:, g, r, :]

    def put_table(first, diffuse, drift_x, drift_y):
        count = diffuse.shape[0]
        parts = (
            1.0 - 4.0 * diffuse,
            diffuse - 0.5 * drift_x,
            diffuse + 0.5 * drift_x,
            diffuse + 0.5 * drift_y,
            diffuse - 0.5 * drift_y,
        )
        for r in range(count):
            for k, part in enumerate(parts):
                table[first + r, k] = jnp.broadcast_to(part[r : r + 1], (SUB, width))

    put_table(STEPS, coef_ref[0], coef_ref[1], coef_ref[2])
    if chunk:
        for first, edge in ((0, above_ref), (STEPS + rows, below_ref)):
            for r in range(STEPS):
                field[first + r] = edge[r, :members, :]
                put_table(
                    first + r,
                    edge[r, members : members + 1, :],
                    edge[r, members + 1 : members + 2, :],
                    edge[r, members + 2 : members + 3, :],
                )

    for shift in range(n_mem):
        group = lax.rem(place[0] + shift, n_mem)
        if chunk:
            start = jnp.where(group == 0, 0, group * SUB + STEPS)
        else:
            start = jnp.where(group == 0, STEPS, group * SUB)

        def some_members(b, carry, start=start, out=outs[shift]):
            at = pl.ds(pl.multiple_of(b * SUB, SUB), SUB)
            now = [field[start + i, at, :] for i in range(HALF + 2 * STEPS)]
            for step in range(STEPS):
                after = []
                for i in range(1, len(now) - 1):
                    row = start + step + i
                    center = now[i]
                    east = pltpu.roll(center, width - 1, 1)
                    west = pltpu.roll(center, 1, 1)
                    after.append(
                        (center * table[row, 0] + east * table[row, 1])
                        + (west * table[row, 2] + now[i - 1] * table[row, 3])
                        + now[i + 1] * table[row, 4]
                    )
                now = after
            for i in range(HALF):
                out[i, at, :] = now[i]
            return carry

        lax.fori_loop(0, members // SUB, some_members, 0)


def forecast(chunk, n_mem, place, ens, coefs, halos=()):
    members, groups, _, width = ens.shape
    rows = groups * SUB
    shape = jax.ShapeDtypeStruct((HALF, members, width), F32)
    return pl.pallas_call(
        functools.partial(forecast_kernel, chunk, n_mem),
        in_specs=[SMEM] + [VMEM] * (2 + len(halos)),
        out_specs=[VMEM] * n_mem,
        out_shape=[shape] * n_mem,
        scratch_shapes=[
            pltpu.VMEM((rows + 2 * STEPS, members, width), F32),
            pltpu.VMEM((rows + 2 * STEPS, 5, SUB, width), F32),
        ],
        name=f"forecast{chunk}",
    )(place, ens, coefs, *halos)


def tally_kernel(value_ref, weight_ref, slab_ref, cell_ref, out_ref):
    blocks, lanes = value_ref.shape
    bins = out_ref.shape[1]
    width = out_ref.shape[2]
    bin_id = lax.broadcasted_iota(jnp.int32, (bins, lanes), 0)
    column_id = lax.broadcasted_iota(jnp.int32, (width, lanes), 0)
    totals = jnp.zeros((2 * bins, width), F32)
    for b in range(blocks):
        cell = cell_ref[b : b + 1, :]
        weight = weight_ref[b : b + 1, :]
        product = weight * value_ref[b : b + 1, :]
        named = slab_ref[b : b + 1, :] * SUB + cell // width
        here = bin_id == named
        column = jnp.where(column_id == cell % width, 1.0, 0.0).astype(BF16)
        rest = jnp.concatenate(
            [jnp.where(here, weight, 0.0), jnp.where(here, product, 0.0)], axis=0
        )
        for _ in range(3):
            piece = rest.astype(BF16)
            rest = rest - piece.astype(F32)
            totals = totals + lax.dot_general(
                piece, column, (((1,), (1,)), ((), ())), preferred_element_type=F32
            )
    out_ref[0] = totals[:bins]
    out_ref[1] = totals[bins:]


def tally(value, weight, slab, cell, n_slab, width):
    lanes = 128
    return pl.pallas_call(
        tally_kernel,
        in_specs=[VMEM] * 4,
        out_specs=VMEM,
        out_shape=jax.ShapeDtypeStruct((2, n_slab * SUB, width), F32),
        name="tally",
    )(*(a.reshape(-1, lanes) for a in (value, weight, slab, cell)))


def halves(a):
    high = a.astype(BF16)
    return high, (a - high.astype(F32)).astype(BF16)


def left(a):
    return jnp.concatenate(halves(a), axis=1)


def right(b):
    both = jnp.concatenate(halves(b), axis=1)
    return jnp.concatenate([both, both], axis=0)


def product(a, b):
    both = jnp.dot(a, b, preferred_element_type=F32)
    width = both.shape[1] // 2
    return both[:, :width] + both[:, width:]


def analyse_kernel(chunk, n_mem, place, tallies_ref, *refs):
    fields, outs, spread = refs[:n_mem], refs[n_mem : 2 * n_mem], refs[2 * n_mem]
    local, width = fields[0].shape[1:]
    members = n_mem * local
    n_slab = tallies_ref.shape[0]
    eye = lax.broadcasted_iota(jnp.int32, (width, width), 0) == lax.broadcasted_iota(
        jnp.int32, (width, width), 1
    )
    total = tallies_ref[0]
    for k in range(1, n_slab):
        total = total + tallies_ref[k]
    first_half = (place[0] == 0) if chunk else (place[0] != 0)
    total = jnp.where(first_half, total[:, :HALF], total[:, HALF:])
    patches = range(HALF)

    means, grams, iterates, scales, gaps = [], [], [], [], []
    for p in patches:
        weight = total[0, p : p + 1, :]
        mean = sum(jnp.sum(f[p], axis=0, keepdims=True) for f in fields) * (1.0 / members)
        for k, f in enumerate(fields):
            spread[p, k * local : (k + 1) * local, :] = (f[p] - mean).astype(BF16)
        s = spread[p]
        gram = lax.dot_general(s, s, (((0,), (0,)), ((), ())), preferred_element_type=F32)
        scaled = gram * weight
        trace = jnp.sum(jnp.where(eye, scaled, 0.0), keepdims=True)
        square = jnp.sum(scaled * scaled.T, keepdims=True)
        norm = (members - 1.0) ** 2 * members + 2.0 * (members - 1.0) * trace + square
        scale = 8.0 * jnp.sqrt(norm * (1.0 / members))
        inverse = 1.0 / scale
        iterates.append(scaled * inverse + jnp.where(eye, (members - 1.0) * inverse, 0.0))
        means.append(mean)
        grams.append(gram)
        scales.append(inverse)
        gaps.append(total[1, p : p + 1, :] - weight * mean)

    roots = [None] * HALF
    for step in range(NS_STEPS):
        last = step == NS_STEPS - 1
        if step == 0:
            both = iterates
        else:
            rights = [right(y) for y in iterates]
            both = [product(left(roots[p]), rights[p]) for p in patches]
        factors = [jnp.where(eye, 1.5, 0.0) - 0.5 * b for b in both]
        lefts = [left(f) for f in factors]
        if not last:
            iterates = [
                product(lefts[p], right(iterates[p]) if step == 0 else rights[p]) for p in patches
            ]
        if step == 0:
            roots = factors
        else:
            roots = [product(lefts[p], right(roots[p])) for p in patches]

    for p in patches:
        root = right(roots[p])
        line = jnp.broadcast_to(gaps[p], (SUB, width))
        line = product(left(line), root)
        line = product(left(line), root)
        line = product(left(line), right(grams[p]))
        base = means[p] + line[:1] * scales[p]
        transform = (jnp.sqrt((members - 1.0) * scales[p]) * roots[p]).astype(BF16)
        update = lax.dot_general(
            spread[p], transform, (((1,), (1,)), ((), ())), preferred_element_type=F32
        )
        for k, out in enumerate(outs):
            out[p] = base + update[k * local : (k + 1) * local]


def analyse(chunk, n_mem, place, tallies, fields):
    shape = jax.ShapeDtypeStruct(fields[0].shape, F32)
    local, width = fields[0].shape[1:]
    return pl.pallas_call(
        functools.partial(analyse_kernel, chunk, n_mem),
        in_specs=[SMEM] + [VMEM] * (1 + n_mem),
        out_specs=[VMEM] * n_mem,
        out_shape=[shape] * n_mem,
        scratch_shapes=[pltpu.VMEM((HALF, n_mem * local, width), BF16)],
        name=f"analyse{chunk}",
    )(place, tallies, *fields)


def gather_kernel(n_mem, place, *refs):
    early, late, out_ref = refs[:n_mem], refs[n_mem : 2 * n_mem], refs[2 * n_mem]
    for shift in range(n_mem):
        group = lax.rem(place[0] + shift, n_mem)
        for r in range(HALF):
            a, b = early[shift][r], late[shift][r]
            out_ref[:, group, r, :] = jnp.where(group == 0, b, a)
            out_ref[:, group, HALF + r, :] = jnp.where(group == 0, a, b)


def gather(n_mem, place, early, late):
    local, width = early[0].shape[1:]
    block = min(local, 2 * SUB)
    part = pl.BlockSpec((HALF, block, width), lambda i: (0, i, 0))
    return pl.pallas_call(
        functools.partial(gather_kernel, n_mem),
        grid=(local // block,),
        in_specs=[SMEM] + [part] * (2 * n_mem),
        out_specs=pl.BlockSpec((block, n_mem, SUB, width), lambda i: (i, 0, 0, 0)),
        out_shape=jax.ShapeDtypeStruct((local, n_mem, SUB, width), F32),
        name="gather",
    )(place, *early, *late)


def shards(ensemble, diffusivity, velocity, obs_value, obs_weight, obs_slab, obs_cell):
    n_slab, n_mem = lax.axis_size("slab"), lax.axis_size("mem")
    members, rows, width = ensemble.shape
    place = lax.axis_index("mem").reshape(1)
    ens = ensemble.reshape(members, n_mem, rows // n_mem, width)
    coefs = jnp.concatenate([diffusivity[None], velocity], axis=0)
    up = [(i, (i + 1) % n_slab) for i in range(n_slab)]
    down = [(j, i) for i, j in up]

    def send(parts, sign):
        moved = [parts[0]]
        for shift in range(1, n_mem):
            ways = [(i, (i + sign * shift) % n_mem) for i in range(n_mem)]
            moved.append(lax.ppermute(parts[shift], "mem", ways))
        return moved

    head, tail = edges(ens, coefs)
    above = lax.ppermute(tail, "slab", up)
    below = lax.ppermute(head, "slab", down)
    early = send(forecast(0, n_mem, place, ens, coefs), 1)
    counts = tally(obs_value, obs_weight, obs_slab, obs_cell, n_slab, width)
    counts = counts.reshape(2, n_slab, SUB, width).transpose(1, 0, 2, 3)
    counts = lax.all_to_all(counts, "slab", split_axis=0, concat_axis=0, tiled=True)
    late = send(forecast(1, n_mem, place, ens, coefs, (above, below)), 1)
    early = send(analyse(0, n_mem, place, counts, early), -1)
    late = send(analyse(1, n_mem, place, counts, late), -1)
    return gather(n_mem, place, early, late).reshape(members, rows, width)


def solution(mesh):
    return jax.shard_map(
        shards,
        mesh=mesh,
        in_specs=(
            P("mem", "slab", None),
            P("slab", None),
            P(None, "slab", None),
            P(("mem", "slab")),
            P(("mem", "slab")),
            P(("mem", "slab"), None),
            P(("mem", "slab")),
        ),
        out_specs=P("mem", "slab", None),
        check_vma=False,
    )
```

```python
import functools

import jax
import jax.numpy as jnp
from jax import lax
from jax.experimental import pallas as pl
from jax.experimental.pallas import tpu as pltpu
from jax.sharding import PartitionSpec as P

STEPS = 4
NS_STEPS = 5
HALF = 4
SUB = 8
F32 = jnp.float32
BF16 = jnp.bfloat16

VMEM = pl.BlockSpec(memory_space=pltpu.VMEM)
SMEM = pl.BlockSpec(memory_space=pltpu.SMEM)


def forecast_kernel(chunk, n_mem, *refs):
    place, ens_ref, diffuse_ref, drift_ref = refs[:4]
    if chunk:
        halos, refs = ((0, refs[4]), (1, refs[5])), refs[6:]
    else:
        edges, refs = refs[4:6], refs[6:]
    outs, (field, table, ping, pong) = refs[:n_mem], refs[n_mem:]
    rows, width = diffuse_ref.shape
    members = ens_ref.shape[0] // rows

    for r in range(rows):
        field[STEPS + r] = ens_ref[pl.ds(r, members, stride=rows), :]

    def put_table(row, diffuse, drift_x, drift_y):
        parts = (
            1.0 - 4.0 * diffuse,
            diffuse - 0.5 * drift_x,
            diffuse + 0.5 * drift_x,
            diffuse + 0.5 * drift_y,
            diffuse - 0.5 * drift_y,
        )
        for k, part in enumerate(parts):
            for r in range(part.shape[0]):
                table[row + r, k] = jnp.broadcast_to(part[r : r + 1], (SUB, width))

    put_table(STEPS, diffuse_ref[...], drift_ref[0], drift_ref[1])
    if chunk:
        for below, halo in halos:
            for r in range(STEPS):
                row = r + below * (STEPS + rows)
                field[row] = halo[r, :members, :]
                put_table(row, *(halo[r, members + k : members + k + 1, :] for k in range(3)))
    else:
        for edge, first in zip(edges, (0, rows - STEPS)):
            for r in range(STEPS):
                row = first + r
                edge[r, :members, :] = field[STEPS + row]
                edge[r, members : members + 1, :] = diffuse_ref[row : row + 1, :]
                for k in range(2):
                    edge[r, members + 1 + k : members + 2 + k, :] = drift_ref[k, row : row + 1, :]

    for shift in range(n_mem):
        group = lax.rem(place[0] + shift, n_mem)
        if chunk:
            start = jnp.where(group == 0, 0, group * SUB + STEPS)
        else:
            start = jnp.where(group == 0, STEPS, group * SUB)
        for step in range(STEPS):
            source = field.at[pl.ds(start, HALF + 2 * STEPS)] if step == 0 else (pong, ping)[step % 2]
            target = outs[shift] if step == STEPS - 1 else (ping, pong)[step % 2]
            for i in range(HALF + 2 * (STEPS - 1 - step)):
                coef = [table[start + step + 1 + i, k] for k in range(5)]
                for m in range(0, members, SUB):
                    at = pl.ds(m, SUB)
                    center = source[i + 1, at, :]
                    target[i, at, :] = (
                        (center * coef[0] + pltpu.roll(center, width - 1, 1) * coef[1])
                        + (pltpu.roll(center, 1, 1) * coef[2] + source[i, at, :] * coef[3])
                        + source[i + 2, at, :] * coef[4]
                    )


def forecast(chunk, n_mem, place, ens, diffusivity, velocity, halos=()):
    rows, width = diffusivity.shape
    members = ens.shape[0] // rows
    part = jax.ShapeDtypeStruct((HALF, members, width), F32)
    edge = jax.ShapeDtypeStruct((STEPS, members + SUB, width), F32)
    shapes = ([] if chunk else [edge] * 2) + [part] * n_mem
    outs = pl.pallas_call(
        functools.partial(forecast_kernel, chunk, n_mem),
        in_specs=[SMEM] + [VMEM] * (3 + len(halos)),
        out_specs=[VMEM] * len(shapes),
        out_shape=shapes,
        scratch_shapes=[
            pltpu.VMEM((rows + 2 * STEPS, members, width), F32),
            pltpu.VMEM((rows + 2 * STEPS, 5, SUB, width), F32),
            pltpu.VMEM((HALF + 2 * STEPS, members, width), F32),
            pltpu.VMEM((HALF + 2 * STEPS, members, width), F32),
        ],
        name=f"forecast{chunk}",
    )(place, ens, diffusivity, velocity, *halos)
    return outs[: len(outs) - n_mem], outs[len(outs) - n_mem :]


def tally_kernel(value_ref, weight_ref, slab_ref, cell_ref, out_ref):
    blocks, lanes = value_ref.shape
    n_slab = out_ref.shape[0]
    width = out_ref.shape[-1]
    bins = n_slab * SUB
    bin_id = lax.broadcasted_iota(jnp.int32, (bins, lanes), 0)
    column_id = lax.broadcasted_iota(jnp.int32, (width, lanes), 0)
    totals = jnp.zeros((2 * bins, width), F32)
    for b in range(blocks):
        cell = cell_ref[b : b + 1, :]
        weight = weight_ref[b : b + 1, :]
        product = weight * value_ref[b : b + 1, :]
        named = slab_ref[b : b + 1, :] * SUB + cell // width
        here = bin_id == named
        column = jnp.where(column_id == cell % width, 1.0, 0.0).astype(BF16)
        rest = jnp.concatenate(
            [jnp.where(here, weight, 0.0), jnp.where(here, product, 0.0)], axis=0
        )
        for _ in range(3):
            piece = rest.astype(BF16)
            rest = rest - piece.astype(F32)
            totals = totals + lax.dot_general(
                piece, column, (((1,), (1,)), ((), ())), preferred_element_type=F32
            )
    for k in range(2 * n_slab):
        out_ref[k % n_slab, k // n_slab] = totals[k * SUB : (k + 1) * SUB]


def tally(value, weight, slab, cell, n_slab, width):
    lanes = 128
    return pl.pallas_call(
        tally_kernel,
        in_specs=[VMEM] * 4,
        out_specs=VMEM,
        out_shape=jax.ShapeDtypeStruct((n_slab, 2, SUB, width), F32),
        name="tally",
    )(*(a.reshape(-1, lanes) for a in (value, weight, slab, cell)))


def halves(a):
    high = a.astype(BF16)
    return high, (a - high.astype(F32)).astype(BF16)


def left(a):
    return jnp.concatenate(halves(a), axis=1)


def right(b):
    both = jnp.concatenate(halves(b), axis=1)
    return jnp.concatenate([both, both], axis=0)


def product(a, b):
    both = jnp.dot(a, b, preferred_element_type=F32)
    width = both.shape[1] // 2
    return both[:, :width] + both[:, width:]


def analyse_kernel(chunk, n_mem, place, tallies_ref, *refs):
    fields, outs, spread = refs[:n_mem], refs[n_mem : 2 * n_mem], refs[2 * n_mem]
    local, width = fields[0].shape[1:]
    members = n_mem * local
    n_slab = tallies_ref.shape[0]
    eye = lax.broadcasted_iota(jnp.int32, (width, width), 0) == lax.broadcasted_iota(
        jnp.int32, (width, width), 1
    )
    total = tallies_ref[0]
    for k in range(1, n_slab):
        total = total + tallies_ref[k]
    first_half = (place[0] == 0) if chunk else (place[0] != 0)
    total = jnp.where(first_half, total[:, :HALF], total[:, HALF:])
    patches = range(HALF)

    means, grams, iterates, scales, gaps = [], [], [], [], []
    for p in patches:
        weight = total[0, p : p + 1, :]
        mean = sum(jnp.sum(f[p], axis=0, keepdims=True) for f in fields) * (1.0 / members)
        for k, f in enumerate(fields):
            spread[p, k * local : (k + 1) * local, :] = (f[p] - mean).astype(BF16)
        s = spread[p]
        gram = lax.dot_general(s, s, (((0,), (0,)), ((), ())), preferred_element_type=F32)
        scaled = gram * weight
        trace = jnp.sum(jnp.where(eye, scaled, 0.0), keepdims=True)
        square = jnp.sum(scaled * scaled.T, keepdims=True)
        norm = (members - 1.0) ** 2 * members + 2.0 * (members - 1.0) * trace + square
        scale = 8.0 * jnp.sqrt(norm * (1.0 / members))
        inverse = 1.0 / scale
        iterates.append(scaled * inverse + jnp.where(eye, (members - 1.0) * inverse, 0.0))
        means.append(mean)
        grams.append(gram)
        scales.append(inverse)
        gaps.append(total[1, p : p + 1, :] - weight * mean)

    roots = [None] * HALF
    for step in range(NS_STEPS):
        last = step == NS_STEPS - 1
        if step == 0:
            both = iterates
        else:
            rights = [right(y) for y in iterates]
            both = [product(left(roots[p]), rights[p]) for p in patches]
        factors = [jnp.where(eye, 1.5, 0.0) - 0.5 * b for b in both]
        lefts = [left(f) for f in factors]
        if not last:
            iterates = [
                product(lefts[p], right(iterates[p]) if step == 0 else rights[p]) for p in patches
            ]
        if step == 0:
            roots = factors
        else:
            roots = [product(lefts[p], right(roots[p])) for p in patches]

    for p in patches:
        root = right(roots[p])
        line = jnp.broadcast_to(gaps[p], (SUB, width))
        line = product(left(line), root)
        line = product(left(line), root)
        line = product(left(line), right(grams[p]))
        base = means[p] + line[:1] * scales[p]
        transform = (jnp.sqrt((members - 1.0) * scales[p]) * roots[p]).astype(BF16)
        update = lax.dot_general(
            spread[p], transform, (((1,), (1,)), ((), ())), preferred_element_type=F32
        )
        for k, out in enumerate(outs):
            out[p] = base + update[k * local : (k + 1) * local]


def analyse(chunk, n_mem, place, tallies, fields):
    shape = jax.ShapeDtypeStruct(fields[0].shape, F32)
    local, width = fields[0].shape[1:]
    return pl.pallas_call(
        functools.partial(analyse_kernel, chunk, n_mem),
        in_specs=[SMEM] + [VMEM] * (1 + n_mem),
        out_specs=[VMEM] * n_mem,
        out_shape=[shape] * n_mem,
        scratch_shapes=[pltpu.VMEM((HALF, n_mem * local, width), BF16)],
        name=f"analyse{chunk}",
    )(place, tallies, *fields)


def gather_kernel(n_mem, place, *refs):
    early, late, out_ref = refs[:n_mem], refs[n_mem : 2 * n_mem], refs[2 * n_mem]
    rows = n_mem * SUB
    members = out_ref.shape[0] // rows
    for shift in range(n_mem):
        group = lax.rem(place[0] + shift, n_mem)
        first = group == 0
        for r in range(HALF):
            a, b = early[shift][r], late[shift][r]
            start = group * SUB + r
            out_ref[pl.ds(start, members, stride=rows), :] = jnp.where(first, b, a)
            out_ref[pl.ds(start + HALF, members, stride=rows), :] = jnp.where(first, a, b)


def gather(n_mem, place, early, late):
    local, width = early[0].shape[1:]
    block = min(local, 2 * SUB)
    rows = n_mem * SUB
    part = pl.BlockSpec((HALF, block, width), lambda i: (0, i, 0))
    return pl.pallas_call(
        functools.partial(gather_kernel, n_mem),
        grid=(local // block,),
        in_specs=[SMEM] + [part] * (2 * n_mem),
        out_specs=pl.BlockSpec((block * rows, width), lambda i: (i, 0)),
        out_shape=jax.ShapeDtypeStruct((local * rows, width), F32),
        name="gather",
    )(place, *early, *late)


def shards(ensemble, diffusivity, velocity, obs_value, obs_weight, obs_slab, obs_cell):
    n_slab, n_mem = lax.axis_size("slab"), lax.axis_size("mem")
    members, rows, width = ensemble.shape
    place = lax.axis_index("mem").reshape(1)
    ens = ensemble.reshape(members * rows, width)
    assert rows == n_mem * SUB
    up = [(i, (i + 1) % n_slab) for i in range(n_slab)]
    down = [(j, i) for i, j in up]

    def send(parts, sign):
        moved = [parts[0]]
        for shift in range(1, n_mem):
            ways = [(i, (i + sign * shift) % n_mem) for i in range(n_mem)]
            moved.append(lax.ppermute(parts[shift], "mem", ways))
        return moved

    (head, tail), early = forecast(0, n_mem, place, ens, diffusivity, velocity)
    above = lax.ppermute(tail, "slab", up)
    below = lax.ppermute(head, "slab", down)
    early = send(early, 1)
    counts = tally(obs_value, obs_weight, obs_slab, obs_cell, n_slab, width)
    counts = lax.all_to_all(counts, "slab", split_axis=0, concat_axis=0, tiled=True)
    _, late = forecast(1, n_mem, place, ens, diffusivity, velocity, (above, below))
    late = send(late, 1)
    early = send(analyse(0, n_mem, place, counts, early), -1)
    late = send(analyse(1, n_mem, place, counts, late), -1)
    return gather(n_mem, place, early, late).reshape(members, rows, width)


def solution(mesh):
    return jax.shard_map(
        shards,
        mesh=mesh,
        in_specs=(
            P("mem", "slab", None),
            P("slab", None),
            P(None, "slab", None),
            P(("mem", "slab")),
            P(("mem", "slab")),
            P(("mem", "slab"), None),
            P(("mem", "slab")),
        ),
        out_specs=P("mem", "slab", None),
        check_vma=False,
    )
```

```python
import functools

import jax
import jax.numpy as jnp
from jax import lax
from jax.experimental import pallas as pl
from jax.experimental.pallas import tpu as pltpu
from jax.sharding import PartitionSpec as P

STEPS = 4
NS_STEPS = 5
HALF = 4
SUB = 8
F32 = jnp.float32
BF16 = jnp.bfloat16

VMEM = pl.BlockSpec(memory_space=pltpu.VMEM)
SMEM = pl.BlockSpec(memory_space=pltpu.SMEM)
HBM = pl.BlockSpec(memory_space=pl.ANY)
PARAMS = pltpu.CompilerParams(vmem_limit_bytes=16 << 20)


def near(arrays):
    return [pltpu.with_memory_space_constraint(a, pltpu.VMEM) for a in arrays]


def put_table(table, row, diffuse, drift_x, drift_y):
    width = diffuse.shape[-1]
    parts = (
        1.0 - 4.0 * diffuse,
        diffuse - 0.5 * drift_x,
        diffuse + 0.5 * drift_x,
        diffuse + 0.5 * drift_y,
        diffuse - 0.5 * drift_y,
    )
    for k, part in enumerate(parts):
        for r in range(part.shape[0]):
            table[row + r, k] = jnp.broadcast_to(part[r : r + 1], (SUB, width))


def advance(field, scratch, table, first, count):
    members, width = field.shape[1:]
    source = field
    for step in range(STEPS):
        target = scratch[step % 2]
        for i in range(first + step + 1, first + count - step - 1):
            coef = [table[i, k] for k in range(5)]
            for m in range(0, members, SUB):
                at = pl.ds(m, SUB)
                center = source[i, at, :]
                target[i, at, :] = (
                    (center * coef[0] + pltpu.roll(center, width - 1, 1) * coef[1])
                    + (pltpu.roll(center, 1, 1) * coef[2] + source[i - 1, at, :] * coef[3])
                    + source[i + 1, at, :] * coef[4]
                )
        source = target
    return source


def inner_kernel(n_mem, *refs):
    place, ens_ref, diffuse_ref, drift_ref = refs[:4]
    edges, early, late = refs[4:6], refs[6 : 6 + n_mem], refs[6 + n_mem : 6 + 2 * n_mem]
    field, table, ping, pong = refs[6 + 2 * n_mem :]
    rows, width = diffuse_ref.shape
    members = ens_ref.shape[0] // rows

    for r in range(rows):
        field[r] = ens_ref[pl.ds(r, members, stride=rows), :]
    put_table(table, 0, diffuse_ref[...], drift_ref[0], drift_ref[1])
    for edge, first in zip(edges, (0, rows - STEPS)):
        for r in range(STEPS):
            row = first + r
            edge[r, :members, :] = field[row]
            edge[r, members : members + 1, :] = diffuse_ref[row : row + 1, :]
            for k in range(2):
                edge[r, members + 1 + k : members + 2 + k, :] = drift_ref[k, row : row + 1, :]

    done = advance(field, (ping, pong), table, 0, rows)
    for shift in range(n_mem):
        group = lax.rem(place[0] + shift, n_mem)
        top = group * SUB + jnp.where(group == 0, HALF, 0)
        bottom = jnp.minimum(group * SUB + HALF, rows - 2 * HALF)
        for r in range(HALF):
            early[shift][r] = done[top + r]
            late[shift][r] = done[bottom + r]


def inner(n_mem, place, ens, diffusivity, velocity):
    rows, width = diffusivity.shape
    members = ens.shape[0] // rows
    part = pltpu.VMEM((HALF, members, width), F32)
    edge = pltpu.VMEM((STEPS, members + SUB, width), F32)
    shapes = [edge] * 2 + [part] * (2 * n_mem)
    outs = pl.pallas_call(
        functools.partial(inner_kernel, n_mem),
        in_specs=[SMEM] + [VMEM] * 3,
        out_specs=[VMEM] * len(shapes),
        out_shape=shapes,
        scratch_shapes=[
            pltpu.VMEM((rows, members, width), F32),
            pltpu.VMEM((rows, 5, SUB, width), F32),
            pltpu.VMEM((rows, members, width), F32),
            pltpu.VMEM((rows, members, width), F32),
        ],
        compiler_params=PARAMS,
        name="inner",
    )(place, ens, diffusivity, velocity)
    return outs[:2], outs[2 : 2 + n_mem], outs[2 + n_mem :]


def outer_kernel(n_mem, *refs):
    place, top_ref, bottom_ref, diffuse_ref, drift_ref, above, below = refs[:7]
    outs = refs[7 + n_mem : 7 + 2 * n_mem]
    field, table, ping, pong = refs[7 + 2 * n_mem :]
    rows = diffuse_ref.shape[0]
    members = field.shape[1]
    span = 3 * STEPS
    lows = (0, rows - 2 * STEPS)

    for side, ref in enumerate((top_ref, bottom_ref)):
        halo = (above, below)[side]
        inside = side * span + (1 - side) * STEPS
        outside = side * span + side * 2 * STEPS
        part = ref.reshape(members * SUB, ref.shape[-1])
        for r in range(SUB):
            field[inside + r] = part[pl.ds(r, members, stride=SUB), :]
        rows_at = pl.ds(lows[side], SUB)
        put_table(table, inside, diffuse_ref[rows_at], drift_ref[0, rows_at], drift_ref[1, rows_at])
        for r in range(STEPS):
            field[outside + r] = halo[r, :members, :]
            put_table(
                table, outside + r, *(halo[r, members + k : members + k + 1, :] for k in range(3))
            )
        done = advance(field, (ping, pong), table, side * span, span)

    for shift in range(n_mem):
        group = lax.rem(place[0] + shift, n_mem)

        @pl.when((group == 0) | (group == n_mem - 1))
        def _(group=group, shift=shift):
            start = jnp.where(group == 0, 0, span) + STEPS
            for r in range(HALF):
                outs[shift][r] = done[start + r]


def outer(n_mem, place, ens, diffusivity, velocity, halos, late):
    rows, width = diffusivity.shape
    members = ens.shape[0]
    span = 6 * STEPS
    late = near(late)
    block = (members, SUB, width)
    whole = [pl.BlockSpec(a.shape, lambda i, n=a.ndim: (0,) * n) for a in (diffusivity, velocity)]
    return pl.pallas_call(
        functools.partial(outer_kernel, n_mem),
        grid=(1,),
        in_specs=[
            SMEM,
            pl.BlockSpec(block, lambda i: (0, 0, 0)),
            pl.BlockSpec(block, lambda i: (0, rows // SUB - 1, 0)),
        ]
        + whole
        + [VMEM] * (2 + n_mem),
        out_specs=[VMEM] * n_mem,
        out_shape=[pltpu.VMEM(a.shape, F32) for a in late],
        scratch_shapes=[
            pltpu.VMEM((span, members, width), F32),
            pltpu.VMEM((span, 5, SUB, width), F32),
            pltpu.VMEM((span, members, width), F32),
            pltpu.VMEM((span, members, width), F32),
        ],
        input_output_aliases={7 + k: k for k in range(n_mem)},
        compiler_params=PARAMS,
        name="outer",
    )(place, ens, ens, diffusivity, velocity, *near(halos), *late)


def tally_kernel(value_ref, weight_ref, slab_ref, cell_ref, out_ref):
    lanes = out_ref.shape[-1]
    blocks = value_ref.shape[1] // lanes
    n_slab = out_ref.shape[0]
    width = out_ref.shape[-1]
    bins = n_slab * SUB
    bin_id = lax.broadcasted_iota(jnp.int32, (bins, lanes), 0)
    column_id = lax.broadcasted_iota(jnp.int32, (width, lanes), 0)
    totals = jnp.zeros((2 * bins, width), F32)
    for b in range(blocks):
        at = pl.ds(b * lanes, lanes)
        cell = cell_ref[:, at]
        weight = weight_ref[:, at]
        product = weight * value_ref[:, at]
        named = slab_ref[:, at] * SUB + cell // width
        here = bin_id == named
        column = jnp.where(column_id == cell % width, 1.0, 0.0).astype(BF16)
        rest = jnp.concatenate(
            [jnp.where(here, weight, 0.0), jnp.where(here, product, 0.0)], axis=0
        )
        for _ in range(3):
            piece = rest.astype(BF16)
            rest = rest - piece.astype(F32)
            totals = totals + lax.dot_general(
                piece, column, (((1,), (1,)), ((), ())), preferred_element_type=F32
            )
    for k in range(2 * n_slab):
        out_ref[k % n_slab, k // n_slab] = totals[k * SUB : (k + 1) * SUB]


def tally(value, weight, slab, cell, n_slab, width):
    return pl.pallas_call(
        tally_kernel,
        in_specs=[VMEM] * 4,
        out_specs=VMEM,
        out_shape=pltpu.VMEM((n_slab, 2, SUB, width), F32),
        compiler_params=PARAMS,
        name="tally",
    )(*(a.reshape(1, -1) for a in (value, weight, slab, cell)))


def halves(a):
    high = a.astype(BF16)
    return high, (a - high.astype(F32)).astype(BF16)


def left(a):
    return jnp.concatenate(halves(a), axis=1)


def right(b):
    both = jnp.concatenate(halves(b), axis=1)
    return jnp.concatenate([both, both], axis=0)


def product(a, b):
    both = jnp.dot(a, b, preferred_element_type=F32)
    width = both.shape[1] // 2
    return both[:, :width] + both[:, width:]


def analyse_kernel(chunk, n_mem, place, tallies_ref, *refs):
    fields, outs, spread = refs[:n_mem], refs[n_mem : 2 * n_mem], refs[2 * n_mem]
    local, width = fields[0].shape[1:]
    members = n_mem * local
    n_slab = tallies_ref.shape[0]
    eye = lax.broadcasted_iota(jnp.int32, (width, width), 0) == lax.broadcasted_iota(
        jnp.int32, (width, width), 1
    )
    total = tallies_ref[0]
    for k in range(1, n_slab):
        total = total + tallies_ref[k]
    first_half = (place[0] == 0) if chunk else (place[0] != 0)
    total = jnp.where(first_half, total[:, :HALF], total[:, HALF:])
    patches = range(HALF)

    means, grams, iterates, scales, gaps = [], [], [], [], []
    for p in patches:
        weight = total[0, p : p + 1, :]
        mean = sum(jnp.sum(f[p], axis=0, keepdims=True) for f in fields) * (1.0 / members)
        for k, f in enumerate(fields):
            spread[p, k * local : (k + 1) * local, :] = (f[p] - mean).astype(BF16)
        s = spread[p]
        gram = lax.dot_general(s, s, (((0,), (0,)), ((), ())), preferred_element_type=F32)
        scaled = gram * weight
        trace = jnp.sum(jnp.where(eye, scaled, 0.0), keepdims=True)
        square = jnp.sum(scaled * scaled.T, keepdims=True)
        norm = (members - 1.0) ** 2 * members + 2.0 * (members - 1.0) * trace + square
        scale = 8.0 * jnp.sqrt(norm * (1.0 / members))
        inverse = 1.0 / scale
        iterates.append(scaled * inverse + jnp.where(eye, (members - 1.0) * inverse, 0.0))
        means.append(mean)
        grams.append(gram)
        scales.append(inverse)
        gaps.append(total[1, p : p + 1, :] - weight * mean)

    roots = [None] * HALF
    for step in range(NS_STEPS):
        last = step == NS_STEPS - 1
        if step == 0:
            both = iterates
        else:
            rights = [right(y) for y in iterates]
            both = [product(left(roots[p]), rights[p]) for p in patches]
        factors = [jnp.where(eye, 1.5, 0.0) - 0.5 * b for b in both]
        lefts = [left(f) for f in factors]
        if not last:
            iterates = [
                product(lefts[p], right(iterates[p]) if step == 0 else rights[p]) for p in patches
            ]
        if step == 0:
            roots = factors
        else:
            roots = [product(lefts[p], right(roots[p])) for p in patches]

    for p in patches:
        root = right(roots[p])
        line = jnp.broadcast_to(gaps[p], (SUB, width))
        line = product(left(line), root)
        line = product(left(line), root)
        line = product(left(line), right(grams[p]))
        base = means[p] + line[:1] * scales[p]
        transform = (jnp.sqrt((members - 1.0) * scales[p]) * roots[p]).astype(BF16)
        update = lax.dot_general(
            spread[p], transform, (((1,), (1,)), ((), ())), preferred_element_type=F32
        )
        for k, out in enumerate(outs):
            out[pl.ds(p, local, stride=HALF), :] = base + update[k * local : (k + 1) * local]


def analyse(chunk, n_mem, place, tallies, fields):
    local, width = fields[0].shape[1:]
    shape = pltpu.VMEM((local * HALF, width), F32)
    return pl.pallas_call(
        functools.partial(analyse_kernel, chunk, n_mem),
        in_specs=[SMEM] + [VMEM] * (1 + n_mem),
        out_specs=[VMEM] * n_mem,
        out_shape=[shape] * n_mem,
        scratch_shapes=[pltpu.VMEM((HALF, n_mem * local, width), BF16)],
        compiler_params=PARAMS,
        name=f"analyse{chunk}",
    )(place, *near([tallies, *fields]))


def settle_kernel(chunk, n_mem, place, *refs):
    parts, out_ref, sems = refs[:n_mem], refs[-2], refs[-1]
    copies = []
    for shift in range(n_mem):
        group = lax.rem(place[0] + shift, n_mem)
        second = (group != 0) if chunk else (group == 0)
        at = 2 * group + second.astype(jnp.int32)
        copies.append(pltpu.make_async_copy(parts[shift], out_ref.at[:, at], sems.at[shift]))
    for copy in copies:
        copy.start()
    for copy in copies:
        copy.wait()


def settle(chunk, n_mem, place, parts, out=None):
    local, width = parts[0].shape[0] // HALF, parts[0].shape[1]
    parts = near([a.reshape(local, HALF, width) for a in parts])
    return pl.pallas_call(
        functools.partial(settle_kernel, chunk, n_mem),
        in_specs=[SMEM] + [VMEM] * n_mem + [HBM] * chunk,
        out_specs=HBM,
        out_shape=jax.ShapeDtypeStruct((local, 2 * n_mem, HALF, width), F32),
        scratch_shapes=[pltpu.SemaphoreType.DMA((n_mem,))],
        input_output_aliases={1 + n_mem: 0} if chunk else {},
        compiler_params=PARAMS,
        name=f"settle{chunk}",
    )(place, *parts, *([out] if chunk else []))


def shards(ensemble, diffusivity, velocity, obs_value, obs_weight, obs_slab, obs_cell):
    n_slab, n_mem = lax.axis_size("slab"), lax.axis_size("mem")
    members, rows, width = ensemble.shape
    place = lax.axis_index("mem").reshape(1)
    assert rows == n_mem * SUB
    up = [(i, (i + 1) % n_slab) for i in range(n_slab)]
    down = [(j, i) for i, j in up]

    def send(parts, sign):
        moved = [parts[0]]
        for shift in range(1, n_mem):
            ways = [(i, (i + sign * shift) % n_mem) for i in range(n_mem)]
            moved.append(lax.ppermute(parts[shift], "mem", ways))
        return moved

    flat = ensemble.reshape(members * rows, width)
    (head, tail), early, late = inner(n_mem, place, flat, diffusivity, velocity)
    above = lax.ppermute(tail, "slab", up)
    below = lax.ppermute(head, "slab", down)
    early = send(early, 1)
    counts = tally(obs_value, obs_weight, obs_slab, obs_cell, n_slab, width)
    counts = lax.all_to_all(counts, "slab", split_axis=0, concat_axis=0, tiled=True)
    late = outer(n_mem, place, ensemble, diffusivity, velocity, (above, below), late)
    late = send(late, 1)
    early = send(analyse(0, n_mem, place, counts, early), -1)
    late = send(analyse(1, n_mem, place, counts, late), -1)
    out = settle(0, n_mem, place, early)
    return settle(1, n_mem, place, late, out).reshape(members, rows, width)


def solution(mesh):
    return jax.shard_map(
        shards,
        mesh=mesh,
        in_specs=(
            P("mem", "slab", None),
            P("slab", None),
            P(None, "slab", None),
            P(("mem", "slab")),
            P(("mem", "slab")),
            P(("mem", "slab"), None),
            P(("mem", "slab")),
        ),
        out_specs=P("mem", "slab", None),
        check_vma=False,
    )
```

```python
import functools

import jax
import jax.numpy as jnp
from jax import lax
from jax.experimental import pallas as pl
from jax.experimental.pallas import tpu as pltpu
from jax.sharding import PartitionSpec as P


STEPS = 4
NS_STEPS = 5
HALF = 4
SUB = 8
F32 = jnp.float32
BF16 = jnp.bfloat16


VMEM = pl.BlockSpec(memory_space=pltpu.VMEM)
SMEM = pl.BlockSpec(memory_space=pltpu.SMEM)
HBM = pl.BlockSpec(memory_space=pl.ANY)
PARAMS = pltpu.CompilerParams(vmem_limit_bytes=16 << 20)


def near(arrays):
    return [pltpu.with_memory_space_constraint(a, pltpu.VMEM) for a in arrays]


def far(arrays):
    return [pltpu.with_memory_space_constraint(a, pltpu.HBM) for a in arrays]


def put_table(table, row, diffuse, drift_x, drift_y):
    width = diffuse.shape[-1]
    parts = (
        1.0 - 4.0 * diffuse,
        diffuse - 0.5 * drift_x,
        diffuse + 0.5 * drift_x,
        diffuse + 0.5 * drift_y,
        diffuse - 0.5 * drift_y,
    )
    for k, part in enumerate(parts):
        for r in range(part.shape[0]):
            table[row + r, k] = jnp.broadcast_to(part[r : r + 1], (SUB, width))


def advance(field, scratch, table, first, count):
    members, width = field.shape[1:]
    source = field
    for step in range(STEPS):
        target = scratch[step % 2]
        for i in range(first + step + 1, first + count - step - 1):
            coef = [table[i, k] for k in range(5)]
            for m in range(0, members, SUB):
                at = pl.ds(m, SUB)
                center = source[i, at, :]
                target[i, at, :] = (
                    (center * coef[0] + pltpu.roll(center, width - 1, 1) * coef[1])
                    + (pltpu.roll(center, 1, 1) * coef[2] + source[i - 1, at, :] * coef[3])
                    + source[i + 1, at, :] * coef[4]
                )
        source = target
    return source


def inner_kernel(n_mem, *refs):
    place, ens_hbm, diffuse_hbm, drift_hbm = refs[:4]
    edges, early, late = refs[4:6], refs[6 : 6 + n_mem], refs[6 + n_mem : 6 + 2 * n_mem]
    field, table, ping, pong, ens_ref, diffuse_ref, drift_ref, sems = refs[6 + 2 * n_mem :]
    rows, width = diffuse_ref.shape
    members = ens_hbm.shape[0]

    copies = [
        pltpu.make_async_copy(diffuse_hbm, diffuse_ref, sems.at[n_mem]),
        pltpu.make_async_copy(drift_hbm, drift_ref, sems.at[n_mem + 1]),
    ]
    for g in range(n_mem):
        copies.append(
            pltpu.make_async_copy(ens_hbm.at[:, pl.ds(g * SUB, SUB)], ens_ref.at[g], sems.at[g])
        )
    for copy in copies:
        copy.start()
    copies[0].wait()
    copies[1].wait()
    put_table(table, 0, diffuse_ref[...], drift_ref[0], drift_ref[1])
    for g in range(n_mem):
        copies[2 + g].wait()
        group = ens_ref.at[g].reshape(members * SUB, width)
        for r in range(SUB):
            field[g * SUB + r] = group[pl.ds(r, members, stride=SUB), :]
    for edge, first in zip(edges, (0, rows - STEPS)):
        for r in range(STEPS):
            row = first + r
            edge[r, :members, :] = field[row]
            edge[r, members : members + 1, :] = diffuse_ref[row : row + 1, :]
            for k in range(2):
                edge[r, members + 1 + k : members + 2 + k, :] = drift_ref[k, row : row + 1, :]

    done = advance(field, (ping, pong), table, 0, rows)
    for shift in range(n_mem):
        group = lax.rem(place[0] + shift, n_mem)
        top = group * SUB + jnp.where(group == 0, HALF, 0)
        bottom = jnp.minimum(group * SUB + HALF, rows - 2 * HALF)
        for r in range(HALF):
            early[shift][r] = done[top + r]
            late[shift][r] = done[bottom + r]


def inner(n_mem, place, ens, diffusivity, velocity):
    rows, width = diffusivity.shape
    members = ens.shape[0]
    part = pltpu.VMEM((HALF, members, width), F32)
    edge = pltpu.VMEM((STEPS, members + SUB, width), F32)
    shapes = [edge] * 2 + [part] * (2 * n_mem)
    outs = pl.pallas_call(
        functools.partial(inner_kernel, n_mem),
        in_specs=[SMEM] + [HBM] * 3,
        out_specs=[VMEM] * len(shapes),
        out_shape=shapes,
        scratch_shapes=[
            pltpu.VMEM((rows, members, width), F32),
            pltpu.VMEM((rows, 5, SUB, width), F32),
            pltpu.VMEM((rows, members, width), F32),
            pltpu.VMEM((rows, members, width), F32),
            pltpu.VMEM((n_mem, members, SUB, width), F32),
            pltpu.VMEM(diffusivity.shape, F32),
            pltpu.VMEM(velocity.shape, F32),
            pltpu.SemaphoreType.DMA((n_mem + 2,)),
        ],
        compiler_params=PARAMS,
        name="inner",
    )(place, *far([ens, diffusivity, velocity]))
    return outs[:2], outs[2 : 2 + n_mem], outs[2 + n_mem :]


def outer_kernel(n_mem, *refs):
    place, top_ref, bottom_ref, diffuse_ref, drift_ref, above, below = refs[:7]
    outs = refs[7 + n_mem : 7 + 2 * n_mem]
    field, table, ping, pong = refs[7 + 2 * n_mem :]
    rows = diffuse_ref.shape[0]
    members = field.shape[1]
    span = 3 * STEPS
    lows = (0, rows - 2 * STEPS)

    for side, ref in enumerate((top_ref, bottom_ref)):
        halo = (above, below)[side]
        inside = side * span + (1 - side) * STEPS
        outside = side * span + side * 2 * STEPS
        part = ref.reshape(members * SUB, ref.shape[-1])
        for r in range(SUB):
            field[inside + r] = part[pl.ds(r, members, stride=SUB), :]
        rows_at = pl.ds(lows[side], SUB)
        put_table(table, inside, diffuse_ref[rows_at], drift_ref[0, rows_at], drift_ref[1, rows_at])
        for r in range(STEPS):
            field[outside + r] = halo[r, :members, :]
            put_table(
                table, outside + r, *(halo[r, members + k : members + k + 1, :] for k in range(3))
            )
        done = advance(field, (ping, pong), table, side * span, span)

    for shift in range(n_mem):
        group = lax.rem(place[0] + shift, n_mem)

        @pl.when((group == 0) | (group == n_mem - 1))
        def _(group=group, shift=shift):
            start = jnp.where(group == 0, 0, span) + STEPS
            for r in range(HALF):
                outs[shift][r] = done[start + r]


def outer(n_mem, place, ens, diffusivity, velocity, halos, late):
    rows, width = diffusivity.shape
    members = ens.shape[0]
    span = 6 * STEPS
    late = near(late)
    block = (members, SUB, width)
    whole = [pl.BlockSpec(a.shape, lambda i, n=a.ndim: (0,) * n) for a in (diffusivity, velocity)]
    return pl.pallas_call(
        functools.partial(outer_kernel, n_mem),
        grid=(1,),
        in_specs=[
            SMEM,
            pl.BlockSpec(block, lambda i: (0, 0, 0)),
            pl.BlockSpec(block, lambda i: (0, rows // SUB - 1, 0)),
        ]
        + whole
        + [VMEM] * (2 + n_mem),
        out_specs=[VMEM] * n_mem,
        out_shape=[pltpu.VMEM(a.shape, F32) for a in late],
        scratch_shapes=[
            pltpu.VMEM((span, members, width), F32),
            pltpu.VMEM((span, 5, SUB, width), F32),
            pltpu.VMEM((span, members, width), F32),
            pltpu.VMEM((span, members, width), F32),
        ],
        input_output_aliases={7 + k: k for k in range(n_mem)},
        compiler_params=PARAMS,
        name="outer",
    )(place, ens, ens, diffusivity, velocity, *near(halos), *late)


def tally_kernel(*refs):
    out_ref, sems, value_ref, weight_ref, slab_ref, cell_ref = refs[4:]
    copies = [pltpu.make_async_copy(refs[k], refs[6 + k], sems.at[k]) for k in range(4)]
    for copy in copies:
        copy.start()
    for copy in copies:
        copy.wait()
    lanes = out_ref.shape[-1]
    blocks = value_ref.shape[0]
    n_slab = out_ref.shape[0]
    width = out_ref.shape[-1]
    bins = n_slab * SUB
    bin_id = lax.broadcasted_iota(jnp.int32, (bins, lanes), 0)
    column_id = lax.broadcasted_iota(jnp.int32, (width, lanes), 0)
    totals = jnp.zeros((2 * bins, width), F32)
    for b in range(blocks):
        cell = cell_ref[b : b + 1, :]
        weight = weight_ref[b : b + 1, :]
        product = weight * value_ref[b : b + 1, :]
        named = slab_ref[:, pl.ds(b * lanes, lanes)] * SUB + cell // width
        here = bin_id == named
        column = jnp.where(column_id == cell % width, 1.0, 0.0).astype(BF16)
        rest = jnp.concatenate(
            [jnp.where(here, weight, 0.0), jnp.where(here, product, 0.0)], axis=0
        )
        for _ in range(3):
            piece = rest.astype(BF16)
            rest = rest - piece.astype(F32)
            totals = totals + lax.dot_general(
                piece, column, (((1,), (1,)), ((), ())), preferred_element_type=F32
            )
    for k in range(2 * n_slab):
        out_ref[k % n_slab, k // n_slab] = totals[k * SUB : (k + 1) * SUB]


def tally(value, weight, slab, cell, n_slab, width):
    value, weight, cell = (a.reshape(-1, width) for a in (value, weight, cell))
    arrays = [value, weight, slab.reshape(1, -1), cell]
    return pl.pallas_call(
        tally_kernel,
        in_specs=[HBM] * 4,
        out_specs=VMEM,
        out_shape=pltpu.VMEM((n_slab, 2, SUB, width), F32),
        scratch_shapes=[pltpu.SemaphoreType.DMA((4,))]
        + [pltpu.VMEM(a.shape, a.dtype) for a in arrays],
        compiler_params=PARAMS,
        name="tally",
    )(*far(arrays))


def halves(a):
    high = a.astype(BF16)
    return high, (a - high.astype(F32)).astype(BF16)


def left(a):
    return jnp.concatenate(halves(a), axis=1)


def right(b):
    both = jnp.concatenate(halves(b), axis=1)
    return jnp.concatenate([both, both], axis=0)


def product(a, b):
    both = jnp.dot(a, b, preferred_element_type=F32)
    width = both.shape[1] // 2
    return both[:, :width] + both[:, width:]


def analyse_kernel(chunk, n_mem, place, tallies_ref, *refs):
    fields, outs, spread = refs[:n_mem], refs[n_mem : 2 * n_mem], refs[2 * n_mem]
    local, width = fields[0].shape[1:]
    members = n_mem * local
    n_slab = tallies_ref.shape[0]
    eye = lax.broadcasted_iota(jnp.int32, (width, width), 0) == lax.broadcasted_iota(
        jnp.int32, (width, width), 1
    )
    total = tallies_ref[0]
    for k in range(1, n_slab):
        total = total + tallies_ref[k]
    first_half = (place[0] == 0) if chunk else (place[0] != 0)
    total = jnp.where(first_half, total[:, :HALF], total[:, HALF:])
    patches = range(HALF)

    means, grams, iterates, scales, gaps = [], [], [], [], []
    for p in patches:
        weight = total[0, p : p + 1, :]
        mean = sum(jnp.sum(f[p], axis=0, keepdims=True) for f in fields) * (1.0 / members)
        for k, f in enumerate(fields):
            spread[p, k * local : (k + 1) * local, :] = (f[p] - mean).astype(BF16)
        s = spread[p]
        gram = lax.dot_general(s, s, (((0,), (0,)), ((), ())), preferred_element_type=F32)
        scaled = gram * weight
        trace = jnp.sum(jnp.where(eye, scaled, 0.0), keepdims=True)
        square = jnp.sum(scaled * scaled.T, keepdims=True)
        norm = (members - 1.0) ** 2 * members + 2.0 * (members - 1.0) * trace + square
        scale = 8.0 * jnp.sqrt(norm * (1.0 / members))
        inverse = 1.0 / scale
        iterates.append(scaled * inverse + jnp.where(eye, (members - 1.0) * inverse, 0.0))
        means.append(mean)
        grams.append(gram)
        scales.append(inverse)
        gaps.append(total[1, p : p + 1, :] - weight * mean)

    roots = [None] * HALF
    for step in range(NS_STEPS):
        last = step == NS_STEPS - 1
        if step == 0:
            both = iterates
        else:
            rights = [right(y) for y in iterates]
            both = [product(left(roots[p]), rights[p]) for p in patches]
        factors = [jnp.where(eye, 1.5, 0.0) - 0.5 * b for b in both]
        lefts = [left(f) for f in factors]
        if not last:
            iterates = [
                product(lefts[p], right(iterates[p]) if step == 0 else rights[p]) for p in patches
            ]
        if step == 0:
            roots = factors
        else:
            roots = [product(lefts[p], right(roots[p])) for p in patches]

    for p in patches:
        root = right(roots[p])
        line = jnp.broadcast_to(gaps[p], (SUB, width))
        line = product(left(line), root)
        line = product(left(line), root)
        line = product(left(line), right(grams[p]))
        base = means[p] + line[:1] * scales[p]
        transform = (jnp.sqrt((members - 1.0) * scales[p]) * roots[p]).astype(BF16)
        update = lax.dot_general(
            spread[p], transform, (((1,), (1,)), ((), ())), preferred_element_type=F32
        )
        for k, out in enumerate(outs):
            out[pl.ds(p, local, stride=HALF), :] = base + update[k * local : (k + 1) * local]


def analyse(chunk, n_mem, place, tallies, fields):
    local, width = fields[0].shape[1:]
    shape = pltpu.VMEM((local * HALF, width), F32)
    return pl.pallas_call(
        functools.partial(analyse_kernel, chunk, n_mem),
        in_specs=[SMEM] + [VMEM] * (1 + n_mem),
        out_specs=[VMEM] * n_mem,
        out_shape=[shape] * n_mem,
        scratch_shapes=[pltpu.VMEM((HALF, n_mem * local, width), BF16)],
        compiler_params=PARAMS,
    )(place, *near([tallies, *fields]))


def settle_kernel(chunk, n_mem, place, *refs):
    parts, out_ref, sems = refs[:n_mem], refs[-2], refs[-1]
    copies = []
    for shift in range(n_mem):
        group = lax.rem(place[0] + shift, n_mem)
        second = (group != 0) if chunk else (group == 0)
        at = 2 * group + second.astype(jnp.int32)
        copies.append(pltpu.make_async_copy(parts[shift], out_ref.at[:, at], sems.at[shift]))
    for copy in copies:
        copy.start()
    for copy in copies:
        copy.wait()


def settle(chunk, n_mem, place, parts, out=None):
    local, width = parts[0].shape[0] // HALF, parts[0].shape[1]
    parts = near([a.reshape(local, HALF, width) for a in parts])
    return pl.pallas_call(
        functools.partial(settle_kernel, chunk, n_mem),
        in_specs=[SMEM] + [VMEM] * n_mem + [HBM] * chunk,
        out_specs=HBM,
        out_shape=jax.ShapeDtypeStruct((local, 2 * n_mem, HALF, width), F32),
        scratch_shapes=[pltpu.SemaphoreType.DMA((n_mem,))],
        input_output_aliases={1 + n_mem: 0} if chunk else {},
        compiler_params=PARAMS,
    )(place, *parts, *([out] if chunk else []))


def shards(ensemble, diffusivity, velocity, obs_value, obs_weight, obs_slab, obs_cell):
    n_slab, n_mem = lax.axis_size("slab"), lax.axis_size("mem")
    members, rows, width = ensemble.shape
    place = lax.axis_index("mem").reshape(1)
    assert rows == n_mem * SUB
    up = [(i, (i + 1) % n_slab) for i in range(n_slab)]
    down = [(j, i) for i, j in up]

    def send(parts, sign):
        moved = [parts[0]]
        for shift in range(1, n_mem):
            ways = [(i, (i + sign * shift) % n_mem) for i in range(n_mem)]
            moved.append(lax.ppermute(parts[shift], "mem", ways))
        return moved

    (head, tail), early, late = inner(n_mem, place, ensemble, diffusivity, velocity)
    early = send(early, 1)
    above = lax.ppermute(tail, "slab", up)
    below = lax.ppermute(head, "slab", down)
    counts = tally(obs_value, obs_weight, obs_slab, obs_cell, n_slab, width)
    counts = lax.all_to_all(counts, "slab", split_axis=0, concat_axis=0, tiled=True)
    late = outer(n_mem, place, ensemble, diffusivity, velocity, (above, below), late)
    late = send(late, 1)
    early = send(analyse(0, n_mem, place, counts, early), -1)
    late = send(analyse(1, n_mem, place, counts, late), -1)
    out = settle(0, n_mem, place, early)
    return settle(1, n_mem, place, late, out).reshape(members, rows, width)


def solution(mesh):
    return jax.shard_map(
        shards,
        mesh=mesh,
        in_specs=(
            P("mem", "slab", None),
            P("slab", None),
            P(None, "slab", None),
            P(("mem", "slab")),
            P(("mem", "slab")),
            P(("mem", "slab"), None),
            P(("mem", "slab")),
        ),
        out_specs=P("mem", "slab", None),
        check_vma=False,
    )
```

```python
import functools

import jax
import jax.numpy as jnp
from jax import lax
from jax.experimental import pallas as pl
from jax.experimental.pallas import tpu as pltpu
from jax.sharding import PartitionSpec as P


STEPS = 4
NS_STEPS = 5
HALF = 4
SUB = 8
F32 = jnp.float32
BF16 = jnp.bfloat16


VMEM = pl.BlockSpec(memory_space=pltpu.VMEM)
SMEM = pl.BlockSpec(memory_space=pltpu.SMEM)
HBM = pl.BlockSpec(memory_space=pl.ANY)
PARAMS = pltpu.CompilerParams(vmem_limit_bytes=16 << 20)


def near(arrays):
    return [pltpu.with_memory_space_constraint(a, pltpu.VMEM) for a in arrays]


def far(arrays):
    return [pltpu.with_memory_space_constraint(a, pltpu.HBM) for a in arrays]


def put_table(table, row, diffuse, drift_x, drift_y):
    width = diffuse.shape[-1]
    parts = (
        1.0 - 4.0 * diffuse,
        diffuse - 0.5 * drift_x,
        diffuse + 0.5 * drift_x,
        diffuse + 0.5 * drift_y,
        diffuse - 0.5 * drift_y,
    )
    for k, part in enumerate(parts):
        for r in range(part.shape[0]):
            table[row + r, k] = jnp.broadcast_to(part[r : r + 1], (SUB, width))


def advance(field, scratch, table, first, count):
    members, width = field.shape[1:]
    source = field
    for step in range(STEPS):
        target = scratch[step % 2]
        for i in range(first + step + 1, first + count - step - 1):
            coef = [table[i, k] for k in range(5)]
            for m in range(0, members, SUB):
                at = pl.ds(m, SUB)
                center = source[i, at, :]
                target[i, at, :] = (
                    (center * coef[0] + pltpu.roll(center, width - 1, 1) * coef[1])
                    + (pltpu.roll(center, 1, 1) * coef[2] + source[i - 1, at, :] * coef[3])
                    + source[i + 1, at, :] * coef[4]
                )
        source = target
    return source


def tally(value_ref, weight_ref, slab_ref, cell_ref, out_ref):
    n_slab, _, _, width = out_ref.shape
    blocks, lanes = value_ref.shape
    bins = n_slab * SUB
    bin_id = lax.broadcasted_iota(jnp.int32, (bins, lanes), 0)
    column_id = lax.broadcasted_iota(jnp.int32, (width, lanes), 0)
    totals = jnp.zeros((2 * bins, width), F32)
    for b in range(blocks):
        cell = cell_ref[b : b + 1, :]
        weight = weight_ref[b : b + 1, :]
        product = weight * value_ref[b : b + 1, :]
        named = slab_ref[:, pl.ds(b * lanes, lanes)] * SUB + cell // width
        here = bin_id == named
        column = jnp.where(column_id == cell % width, 1.0, 0.0).astype(BF16)
        rest = jnp.concatenate(
            [jnp.where(here, weight, 0.0), jnp.where(here, product, 0.0)], axis=0
        )
        for _ in range(3):
            piece = rest.astype(BF16)
            rest = rest - piece.astype(F32)
            totals = totals + lax.dot_general(
                piece, column, (((1,), (1,)), ((), ())), preferred_element_type=F32
            )
    for k in range(2 * n_slab):
        out_ref[k % n_slab, k // n_slab] = totals[k * SUB : (k + 1) * SUB]


def inner_kernel(n_mem, *refs):
    place, ens_hbm, rest = refs[0], refs[1], refs[2:8]
    refs = refs[8:]
    counts, edges = refs[0], refs[1:3]
    early, late = refs[3 : 3 + n_mem], refs[3 + n_mem : 3 + 2 * n_mem]
    field, table, ping, pong, ens_ref, sems = refs[3 + 2 * n_mem : 9 + 2 * n_mem]
    small = refs[9 + 2 * n_mem :]
    diffuse_ref, drift_ref = small[:2]
    rows, width = diffuse_ref.shape
    members = ens_hbm.shape[0]

    copies = [
        pltpu.make_async_copy(source, target, sems.at[n_mem + k])
        for k, (source, target) in enumerate(zip(rest, small))
    ]
    copies += [
        pltpu.make_async_copy(ens_hbm.at[:, pl.ds(g * SUB, SUB)], ens_ref.at[g], sems.at[g])
        for g in range(n_mem)
    ]
    for copy in copies:
        copy.start()
    for copy in copies[: len(rest)]:
        copy.wait()
    put_table(table, 0, diffuse_ref[...], drift_ref[0], drift_ref[1])
    tally(*small[2:], counts)
    for g in range(n_mem):
        copies[len(rest) + g].wait()
        group = ens_ref.at[g].reshape(members * SUB, width)
        for r in range(SUB):
            field[g * SUB + r] = group[pl.ds(r, members, stride=SUB), :]
    for edge, first in zip(edges, (0, rows - STEPS)):
        for r in range(STEPS):
            row = first + r
            edge[r, :members, :] = field[row]
            edge[r, members : members + 1, :] = diffuse_ref[row : row + 1, :]
            for k in range(2):
                edge[r, members + 1 + k : members + 2 + k, :] = drift_ref[k, row : row + 1, :]

    done = advance(field, (ping, pong), table, 0, rows)
    for shift in range(n_mem):
        group = lax.rem(place[0] + shift, n_mem)
        top = group * SUB + jnp.where(group == 0, HALF, 0)
        bottom = jnp.minimum(group * SUB + HALF, rows - 2 * HALF)
        for r in range(HALF):
            early[shift][r] = done[top + r]
            late[shift][r] = done[bottom + r]


def inner(n_mem, n_slab, place, ens, diffusivity, velocity, value, weight, slab, cell):
    rows, width = diffusivity.shape
    members = ens.shape[0]
    value, weight, cell = (a.reshape(-1, width) for a in (value, weight, cell))
    small = [diffusivity, velocity, value, weight, slab.reshape(1, -1), cell]
    part = pltpu.VMEM((HALF, members, width), F32)
    edge = pltpu.VMEM((STEPS, members + SUB, width), F32)
    shapes = [pltpu.VMEM((n_slab, 2, SUB, width), F32)] + [edge] * 2 + [part] * (2 * n_mem)
    outs = pl.pallas_call(
        functools.partial(inner_kernel, n_mem),
        in_specs=[SMEM] + [HBM] * (1 + len(small)),
        out_specs=[VMEM] * len(shapes),
        out_shape=shapes,
        scratch_shapes=[
            pltpu.VMEM((rows, members, width), F32),
            pltpu.VMEM((rows, 5, SUB, width), F32),
            pltpu.VMEM((rows, members, width), F32),
            pltpu.VMEM((rows, members, width), F32),
            pltpu.VMEM((n_mem, members, SUB, width), F32),
            pltpu.SemaphoreType.DMA((n_mem + len(small),)),
        ]
        + [pltpu.VMEM(a.shape, a.dtype) for a in small],
        compiler_params=PARAMS,
        name="inner",
    )(place, *far([ens, *small]))
    return outs[0], outs[1:3], outs[3 : 3 + n_mem], outs[3 + n_mem :]


def outer_kernel(n_mem, *refs):
    place, top_ref, bottom_ref, diffuse_ref, drift_ref, above, below = refs[:7]
    outs = refs[7 + n_mem : 7 + 2 * n_mem]
    field, table, ping, pong = refs[7 + 2 * n_mem :]
    rows = diffuse_ref.shape[0]
    members = field.shape[1]
    span = 3 * STEPS
    lows = (0, rows - 2 * STEPS)

    for side, ref in enumerate((top_ref, bottom_ref)):
        halo = (above, below)[side]
        inside = side * span + (1 - side) * STEPS
        outside = side * span + side * 2 * STEPS
        part = ref.reshape(members * SUB, ref.shape[-1])
        for r in range(SUB):
            field[inside + r] = part[pl.ds(r, members, stride=SUB), :]
        rows_at = pl.ds(lows[side], SUB)
        put_table(table, inside, diffuse_ref[rows_at], drift_ref[0, rows_at], drift_ref[1, rows_at])
        for r in range(STEPS):
            field[outside + r] = halo[r, :members, :]
            put_table(
                table, outside + r, *(halo[r, members + k : members + k + 1, :] for k in range(3))
            )
        done = advance(field, (ping, pong), table, side * span, span)

    for shift in range(n_mem):
        group = lax.rem(place[0] + shift, n_mem)

        @pl.when((group == 0) | (group == n_mem - 1))
        def _(group=group, shift=shift):
            start = jnp.where(group == 0, 0, span) + STEPS
            for r in range(HALF):
                outs[shift][r] = done[start + r]


def outer(n_mem, place, ens, diffusivity, velocity, halos, late):
    rows, width = diffusivity.shape
    members = ens.shape[0]
    span = 6 * STEPS
    late = near(late)
    block = (members, SUB, width)
    whole = [pl.BlockSpec(a.shape, lambda i, n=a.ndim: (0,) * n) for a in (diffusivity, velocity)]
    return pl.pallas_call(
        functools.partial(outer_kernel, n_mem),
        grid=(1,),
        in_specs=[
            SMEM,
            pl.BlockSpec(block, lambda i: (0, 0, 0)),
            pl.BlockSpec(block, lambda i: (0, rows // SUB - 1, 0)),
        ]
        + whole
        + [VMEM] * (2 + n_mem),
        out_specs=[VMEM] * n_mem,
        out_shape=[pltpu.VMEM(a.shape, F32) for a in late],
        scratch_shapes=[
            pltpu.VMEM((span, members, width), F32),
            pltpu.VMEM((span, 5, SUB, width), F32),
            pltpu.VMEM((span, members, width), F32),
            pltpu.VMEM((span, members, width), F32),
        ],
        input_output_aliases={7 + k: k for k in range(n_mem)},
        compiler_params=PARAMS,
        name="outer",
    )(place, ens, ens, diffusivity, velocity, *near(halos), *late)


def halves(a):
    high = a.astype(BF16)
    return high, (a - high.astype(F32)).astype(BF16)


def left(a):
    return jnp.concatenate(halves(a), axis=1)


def right(b):
    both = jnp.concatenate(halves(b), axis=1)
    return jnp.concatenate([both, both], axis=0)


def product(a, b):
    both = jnp.dot(a, b, preferred_element_type=F32)
    width = both.shape[1] // 2
    return both[:, :width] + both[:, width:]


def analyse_kernel(chunk, n_mem, place, tallies_ref, *refs):
    fields, outs, spread = refs[:n_mem], refs[n_mem : 2 * n_mem], refs[2 * n_mem]
    local, width = fields[0].shape[1:]
    members = n_mem * local
    n_slab = tallies_ref.shape[0]
    eye = lax.broadcasted_iota(jnp.int32, (width, width), 0) == lax.broadcasted_iota(
        jnp.int32, (width, width), 1
    )
    total = tallies_ref[0]
    for k in range(1, n_slab):
        total = total + tallies_ref[k]
    first_half = (place[0] == 0) if chunk else (place[0] != 0)
    total = jnp.where(first_half, total[:, :HALF], total[:, HALF:])
    patches = range(HALF)

    means, grams, iterates, scales, gaps = [], [], [], [], []
    for p in patches:
        weight = total[0, p : p + 1, :]
        mean = sum(jnp.sum(f[p], axis=0, keepdims=True) for f in fields) * (1.0 / members)
        for k, f in enumerate(fields):
            spread[p, k * local : (k + 1) * local, :] = (f[p] - mean).astype(BF16)
        s = spread[p]
        gram = lax.dot_general(s, s, (((0,), (0,)), ((), ())), preferred_element_type=F32)
        scaled = gram * weight
        trace = jnp.sum(jnp.where(eye, scaled, 0.0), keepdims=True)
        square = jnp.sum(scaled * scaled.T, keepdims=True)
        norm = (members - 1.0) ** 2 * members + 2.0 * (members - 1.0) * trace + square
        scale = 8.0 * jnp.sqrt(norm * (1.0 / members))
        inverse = 1.0 / scale
        iterates.append(scaled * inverse + jnp.where(eye, (members - 1.0) * inverse, 0.0))
        means.append(mean)
        grams.append(gram)
        scales.append(inverse)
        gaps.append(total[1, p : p + 1, :] - weight * mean)

    roots = [None] * HALF
    for step in range(NS_STEPS):
        last = step == NS_STEPS - 1
        if step == 0:
            both = iterates
        else:
            rights = [right(y) for y in iterates]
            both = [product(left(roots[p]), rights[p]) for p in patches]
        factors = [jnp.where(eye, 1.5, 0.0) - 0.5 * b for b in both]
        lefts = [left(f) for f in factors]
        if not last:
            iterates = [
                product(lefts[p], right(iterates[p]) if step == 0 else rights[p]) for p in patches
            ]
        if step == 0:
            roots = factors
        else:
            roots = [product(lefts[p], right(roots[p])) for p in patches]

    for p in patches:
        root = right(roots[p])
        line = jnp.broadcast_to(gaps[p], (SUB, width))
        line = product(left(line), root)
        line = product(left(line), root)
        line = product(left(line), right(grams[p]))
        base = means[p] + line[:1] * scales[p]
        transform = (jnp.sqrt((members - 1.0) * scales[p]) * roots[p]).astype(BF16)
        update = lax.dot_general(
            spread[p], transform, (((1,), (1,)), ((), ())), preferred_element_type=F32
        )
        for k, out in enumerate(outs):
            out[pl.ds(p, local, stride=HALF), :] = base + update[k * local : (k + 1) * local]


def analyse(chunk, n_mem, place, tallies, fields):
    local, width = fields[0].shape[1:]
    shape = pltpu.VMEM((local * HALF, width), F32)
    return pl.pallas_call(
        functools.partial(analyse_kernel, chunk, n_mem),
        in_specs=[SMEM] + [VMEM] * (1 + n_mem),
        out_specs=[VMEM] * n_mem,
        out_shape=[shape] * n_mem,
        scratch_shapes=[pltpu.VMEM((HALF, n_mem * local, width), BF16)],
        compiler_params=PARAMS,
    )(place, *near([tallies, *fields]))


def settle_kernel(chunk, n_mem, place, *refs):
    parts, out_ref, sems = refs[:n_mem], refs[-2], refs[-1]
    copies = []
    for shift in range(n_mem):
        group = lax.rem(place[0] + shift, n_mem)
        second = (group != 0) if chunk else (group == 0)
        at = 2 * group + second.astype(jnp.int32)
        copies.append(pltpu.make_async_copy(parts[shift], out_ref.at[:, at], sems.at[shift]))
    for copy in copies:
        copy.start()
    for copy in copies:
        copy.wait()


def settle(chunk, n_mem, place, parts, out=None):
    local, width = parts[0].shape[0] // HALF, parts[0].shape[1]
    parts = near([a.reshape(local, HALF, width) for a in parts])
    return pl.pallas_call(
        functools.partial(settle_kernel, chunk, n_mem),
        in_specs=[SMEM] + [VMEM] * n_mem + [HBM] * chunk,
        out_specs=HBM,
        out_shape=jax.ShapeDtypeStruct((local, 2 * n_mem, HALF, width), F32),
        scratch_shapes=[pltpu.SemaphoreType.DMA((n_mem,))],
        input_output_aliases={1 + n_mem: 0} if chunk else {},
        compiler_params=PARAMS,
    )(place, *parts, *([out] if chunk else []))


def shards(ensemble, diffusivity, velocity, obs_value, obs_weight, obs_slab, obs_cell):
    n_slab, n_mem = lax.axis_size("slab"), lax.axis_size("mem")
    members, rows, width = ensemble.shape
    place = lax.axis_index("mem").reshape(1)
    assert rows == n_mem * SUB
    up = [(i, (i + 1) % n_slab) for i in range(n_slab)]
    down = [(j, i) for i, j in up]

    def send(parts, sign):
        moved = [parts[0]]
        for shift in range(1, n_mem):
            ways = [(i, (i + sign * shift) % n_mem) for i in range(n_mem)]
            moved.append(lax.ppermute(parts[shift], "mem", ways))
        return moved

    counts, (head, tail), early, late = inner(
        n_mem,
        n_slab,
        place,
        ensemble,
        diffusivity,
        velocity,
        obs_value,
        obs_weight,
        obs_slab,
        obs_cell,
    )
    early = send(early, 1)
    above = lax.ppermute(tail, "slab", up)
    below = lax.ppermute(head, "slab", down)
    counts = lax.all_to_all(counts, "slab", split_axis=0, concat_axis=0, tiled=True)
    late = outer(n_mem, place, ensemble, diffusivity, velocity, (above, below), late)
    late = send(late, 1)
    early = send(analyse(0, n_mem, place, counts, early), -1)
    late = send(analyse(1, n_mem, place, counts, late), -1)
    out = settle(0, n_mem, place, early)
    return settle(1, n_mem, place, late, out).reshape(members, rows, width)


def solution(mesh):
    return jax.shard_map(
        shards,
        mesh=mesh,
        in_specs=(
            P("mem", "slab", None),
            P("slab", None),
            P(None, "slab", None),
            P(("mem", "slab")),
            P(("mem", "slab")),
            P(("mem", "slab"), None),
            P(("mem", "slab")),
        ),
        out_specs=P("mem", "slab", None),
        check_vma=False,
    )
```
